32 devices in a mesh: cell: 8 (over z, y), dp: 4 (over x, core).
Axes of the slice: x: 2, y: 2, z: 4, core: 2. Of those that a mesh axis runs over, the one named last changes fastest.
Arguments:
- ensemble: bfloat16 [32768, 512], P('cell'), may hold values from -6 to 6
- response_estimates: float32 [4, 256, 512], P('dp', 'cell'), may hold values from -11 to 11
- observed: float32 [4, 256, 512], P('dp', 'cell'), may hold values from -12 to 12
- obs_std: float32 [4, 256], P('dp', 'cell'), may hold values from 0.2 to 0.5
- threshold: bfloat16 [4, 256], P('dp', 'cell'), may hold values from 0.019897461 to 0.119628906
Outputs:
- updated: float32 [32768, 512], P('cell', 'dp')
- mismatch: float32 [], replicated
The draws below stay inside these ranges and needn't reach their ends.
All inputs are finite; a program needn't handle non-finite values.
Results may differ from the reference program's by a relative error of at most 0.0082.
Values may be sent and summed in bfloat16 or wider, within the bound.
A program may use at most 128 MiB of HBM per device.

```python
import math
import jax
import jax.numpy as jnp
from jax import lax

NE = 512
ND = 1024
CELL_DEV = 4096
CELLS = 32768
DBLK = 256
N_DP = 4


def draw_response_estimates(key, part):
    key_scale = jax.random.fold_in(key, 11)
    key_center = jax.random.fold_in(key, 12)
    key_noise = jax.random.fold_in(key, 13)
    spread_scale = jnp.exp(jax.random.uniform(key_scale, (ND, 1), jnp.float32, math.log(0.02), math.log(4.0)))
    center = jax.random.uniform(key_center, (ND, 1), jnp.float32, -1.0, 1.0)
    fluctuation = jnp.clip(jax.random.normal(key_noise, (ND, NE), jnp.float32), -2.4, 2.4)
    values = center + spread_scale * fluctuation
    return values.reshape(ND // DBLK, DBLK, NE)


def shard_levels(own_key, dims, shards, least, high):
    def one(axis_at, parts):
        heights = jax.random.uniform(jax.random.fold_in(jax.random.fold_in(own_key, 6), axis_at), (parts,), jnp.float32, least / len(shards), high / len(shards))
        return jnp.repeat(jnp.exp(heights), dims[axis_at] // parts).reshape((-1,) + (1,) * (len(dims) - axis_at - 1))

    level = one(*shards[0])
    for cut in shards[1:]:
        level = level * one(*cut)
    return level


def normal_values(key, shape, spread, most, split=(), kind=jnp.bfloat16):
    level = shard_levels(key, shape, split, -0.22, 0.18) if split else 1.0
    drawn = jax.random.normal(key, shape, jnp.float32) * spread * level
    return jnp.minimum(jnp.maximum(drawn, -most), most).astype(kind)


def setup_inputs(seed: int = 0) -> dict:
    keys = jax.random.split(jax.random.key(seed), 6)
    return {
        "ensemble": normal_values(keys[0], (CELLS, NE), 1.0, 6.0, ((0, 8),)),
        "response_estimates": draw_response_estimates(jax.random.fold_in(keys[5], 71), 0),
        "observed": normal_values(keys[2], (N_DP, DBLK, NE), 2.0, 12.0, ((0, 4), (1, 8)), jnp.float32),
        "obs_std": jnp.clip(jnp.exp(math.log(0.5) - 0.9162907 * jax.random.uniform(keys[3], (N_DP, DBLK), jnp.float32) ** shard_levels(keys[3], (N_DP, DBLK), ((0, 4), (1, 8)), -0.2, 0.2)), 0.2, 0.5),
        "threshold": jnp.clip(jnp.exp(math.log(0.119628906) - 1.7938024 * jax.random.uniform(keys[4], (N_DP, DBLK), jnp.float32) ** shard_levels(keys[4], (N_DP, DBLK), ((0, 4), (1, 8)), -0.2, 0.2)), 0.019897461, 0.119628906).astype(jnp.bfloat16),
    }


inflation = 4.0

def reference(ensemble, response_estimates, observed, obs_std, threshold):
    realization_count = ensemble.shape[1]
    background_response = response_estimates.reshape(-1, realization_count)
    measurement_mapping = observed.reshape(-1, realization_count)
    noise = obs_std.reshape(-1)
    limit = threshold.reshape(-1).astype(jnp.float32)
    realization_spread = background_response - lax.optimization_barrier(jnp.mean(background_response, axis=1, keepdims=True))
    datum_scale_factor = jnp.sqrt(lax.optimization_barrier(jnp.mean(realization_spread * realization_spread, axis=1)) + 1e-06)
    unit_data = (realization_spread / (datum_scale_factor[:, None] * math.sqrt(realization_count))).astype(jnp.bfloat16)
    error_covariance_sqrtm = noise * math.sqrt(inflation)
    scaled = realization_spread / (error_covariance_sqrtm[:, None] * math.sqrt(realization_count - 1.0))
    measured_misfit = (measurement_mapping - background_response) / error_covariance_sqrtm[:, None]
    gram_total = jnp.dot(scaled.T, scaled, precision=lax.Precision.HIGHEST)
    projected = jnp.dot(scaled.T, measured_misfit, precision=lax.Precision.HIGHEST)
    mismatch = jnp.mean(measured_misfit * measured_misfit)
    system = jnp.eye(realization_count, dtype=jnp.float32) + gram_total
    factor = jnp.linalg.cholesky(system)
    weights_h = jax.scipy.linalg.cho_solve((factor, True), projected)
    weights = (measured_misfit - jnp.dot(scaled, weights_h, precision=lax.Precision.HIGHEST)) / error_covariance_sqrtm[:, None]
    carried = (datum_scale_factor[:, None] * weights).astype(jnp.bfloat16)

    def update_block(rows_block):
        values = rows_block.astype(jnp.float32)
        anomaly = values - lax.optimization_barrier(jnp.mean(values, axis=1, keepdims=True))
        cell_scale = jnp.sqrt(lax.optimization_barrier(jnp.mean(anomaly * anomaly, axis=1)) + 1e-06)
        unit_cells = (anomaly / (cell_scale[:, None] * math.sqrt(realization_count))).astype(jnp.bfloat16)
        correlate = lax.dot_general(unit_cells.astype(jnp.float32), unit_data.astype(jnp.float32), (((1,), (1,)), ((), ())), preferred_element_type=jnp.float32)
        square = correlate * correlate
        kalman_weighted = (square / (square + limit[None, :] * limit[None, :]) * correlate).astype(jnp.bfloat16)
        increment = jnp.dot(kalman_weighted.astype(jnp.float32), carried.astype(jnp.float32), preferred_element_type=jnp.float32)
        return values + cell_scale[:, None] * (realization_count / (realization_count - 1.0)) * increment
    blocks = ensemble.reshape(-1, CELL_DEV, realization_count)
    updated = lax.map(update_block, blocks).reshape(-1, realization_count)
    return (updated, mismatch)
```

```python
import math

import jax
import jax.numpy as jnp
from jax import lax
from jax.experimental import pallas as pl
from jax.experimental.pallas import tpu as pltpu
from jax.sharding import PartitionSpec as P

inflation = 4.0
LANES = 128
CHECK_EVERY = 3
F32 = jnp.float32
BF16 = jnp.bfloat16


def pieces(x):
    out = []
    for _ in range(3):
        part = lax.reduce_precision(x, 8, 7)
        out.append(part.astype(BF16))
        x = x - part
    return out


def joined(parts, at):
    return (
        parts[:, at].astype(F32) + parts[:, at + 1].astype(F32) + parts[:, at + 2].astype(F32)
    )


def split2(x):
    high = x.astype(BF16)
    return high, (x - high.astype(F32)).astype(BF16)


def tdot(a, b):
    return lax.dot_general(a, b, (((0,), (0,)), ((), ())), preferred_element_type=F32)


def solve_kernel(limit_steps, unit, innovation, ratio, carry, out, s2, a2, work, x, r, p, norms):
    nd, ne = unit.shape
    cols = innovation.shape[1]
    high, low = split2(unit[...].astype(F32) * ratio[...])
    s2[:nd, :] = high
    s2[nd:, :] = low
    cross = tdot(high, low)
    work[...] = cross + cross.T
    work[...] += tdot(high, high)
    for first in range(0, ne, cols):
        rows = pl.ds(first, cols)
        across = lax.broadcasted_iota(jnp.int32, (cols, ne), 1)
        down = lax.broadcasted_iota(jnp.int32, (cols, ne), 0) + first
        block = work[rows, :] + jnp.where(across == down, 1.0, 0.0)
        a_high, a_low = split2(block)
        a2[rows, :] = a_high
        a2[pl.ds(ne + first, cols), :] = a_low
    inn = innovation[...]
    rhs = tdot(high, inn) + tdot(low, inn)
    inn32 = inn.astype(F32)
    goal = jnp.sum(inn32 * inn32, axis=0, keepdims=True) * (2.0**-30)
    x[...] = jnp.zeros_like(x)
    r[...] = rhs
    p[...] = rhs
    rr0 = jnp.sum(rhs * rhs, axis=0, keepdims=True)
    norms[0:1, :] = rr0
    norms[1:2, :] = goal

    def more(state):
        step, worst = state
        return jnp.logical_and(step < limit_steps, worst > 0.0)

    def block(state):
        step, _ = state
        rr = norms[0:1, :]
        for _ in range(CHECK_EVERY):
            p_now = p[...]
            p_high, p_low = split2(p_now)
            both = jnp.dot(
                a2[...], jnp.concatenate([p_high, p_low], axis=1), preferred_element_type=F32
            )
            q = (both[:ne, :cols] + both[:ne, cols:]) + (both[ne:, :cols] + both[ne:, cols:])
            pq = jnp.sum(p_now * q, axis=0, keepdims=True)
            alpha = jnp.where(pq > 0.0, rr / jnp.where(pq > 0.0, pq, 1.0), 0.0)
            x[...] = x[...] + alpha * p_now
            r_new = r[...] - alpha * q
            r[...] = r_new
            rr_new = jnp.sum(r_new * r_new, axis=0, keepdims=True)
            beta = jnp.where(rr > 0.0, rr_new / jnp.where(rr > 0.0, rr, 1.0), 0.0)
            p[...] = r_new + beta * p_now
            rr = rr_new
        norms[0:1, :] = rr
        return step + CHECK_EVERY, jnp.max(rr - norms[1:2, :])

    lax.while_loop(more, block, (jnp.int32(0), jnp.max(rr0 - goal)))
    x_high, x_low = split2(x[...])
    both = jnp.dot(s2[...], jnp.concatenate([x_high, x_low], axis=1), preferred_element_type=F32)
    fitted = (both[:nd, :cols] + both[:nd, cols:]) + (both[nd:, :cols] + both[nd:, cols:])
    out[...] = ((inn32 - fitted) * carry[...]).astype(BF16)


def solve(unit, innovation, ratio, carry):
    nd, ne = unit.shape
    cols = innovation.shape[1]
    vmem = pl.BlockSpec(memory_space=pltpu.VMEM)
    return pl.pallas_call(
        lambda *refs: solve_kernel(8 * ne, *refs),
        out_shape=jax.ShapeDtypeStruct((nd, cols), BF16),
        in_specs=[vmem] * 4,
        out_specs=vmem,
        scratch_shapes=[
            pltpu.VMEM((2 * nd, ne), BF16),
            pltpu.VMEM((2 * ne, ne), BF16),
            pltpu.VMEM((ne, ne), F32),
            pltpu.VMEM((ne, cols), F32),
            pltpu.VMEM((ne, cols), F32),
            pltpu.VMEM((ne, cols), F32),
            pltpu.VMEM((8, cols), F32),
        ],
        compiler_params=pltpu.CompilerParams(vmem_limit_bytes=40 * 2**20),
        name="solve",
    )(unit, innovation, ratio, carry)


def per_device(ensemble, response_estimates, observed, obs_std, threshold):
    ne = ensemble.shape[1]
    forecast = response_estimates[0]
    observe = observed[0]
    noise_root = obs_std[0] * math.sqrt(inflation)
    deviation = forecast - jnp.mean(forecast, axis=1, keepdims=True)
    data_scale = jnp.sqrt(jnp.mean(deviation * deviation, axis=1) + 1e-06)
    unit_data = (deviation / (data_scale[:, None] * math.sqrt(ne))).astype(BF16)
    ratio = data_scale * math.sqrt(ne) / (noise_root * math.sqrt(ne - 1.0))
    carry = data_scale / noise_root
    innovation = (observe - forecast) / noise_root[:, None]
    squares = jnp.sum(innovation * innovation, axis=1)
    meta = jnp.stack(
        pieces(ratio) + pieces(carry) + pieces(squares) + [threshold[0].astype(BF16)], axis=1
    )
    meta = jnp.pad(meta, ((0, 0), (0, LANES - meta.shape[1])))
    payload = jnp.concatenate([unit_data, innovation.astype(BF16), meta], axis=1)
    whole = lax.all_gather(payload, ("cell", "dp"), axis=0, tiled=True)
    nd = whole.shape[0]
    column_count = ne // lax.axis_size("dp")
    first_col = lax.axis_index("dp") * column_count
    unit_all = whole[:, :ne]
    own_innovation = lax.dynamic_slice_in_dim(whole, ne + first_col, column_count, 1)
    parts = whole[:, 2 * ne :]
    mismatch = jnp.sum(joined(parts, 6)) / (nd * ne)
    carried = solve(
        unit_all, own_innovation, joined(parts, 0)[:, None], joined(parts, 3)[:, None]
    )
    limit = parts[:, 9].astype(F32)

    values = ensemble.astype(F32)
    anomaly = values - jnp.mean(values, axis=1, keepdims=True)
    cell_scale = jnp.sqrt(jnp.mean(anomaly * anomaly, axis=1) + 1e-06)
    unit_cells = (anomaly / (cell_scale[:, None] * math.sqrt(ne))).astype(BF16)
    correlate = lax.dot_general(
        unit_cells, unit_all, (((1,), (1,)), ((), ())), preferred_element_type=F32
    )
    square = correlate * correlate
    weighted = (square / (square + (limit * limit)[None, :]) * correlate).astype(BF16)
    increment = jnp.dot(weighted, carried, preferred_element_type=F32)
    own_values = lax.dynamic_slice_in_dim(values, first_col, column_count, 1)
    updated = own_values + cell_scale[:, None] * (ne / (ne - 1.0)) * increment
    return (updated, mismatch)


def solution(mesh):
    return jax.shard_map(
        per_device,
        mesh=mesh,
        in_specs=(
            P("cell", None),
            P("dp", "cell", None),
            P("dp", "cell", None),
            P("dp", "cell"),
            P("dp", "cell"),
        ),
        out_specs=(P("cell", "dp"), P()),
        check_vma=False,
    )
```

```python
import math

import jax
import jax.numpy as jnp
from jax import lax
from jax.experimental import pallas as pl
from jax.experimental.pallas import tpu as pltpu
from jax.sharding import PartitionSpec as P

inflation = 4.0
LANES = 128
CHECK_EVERY = 3
F32 = jnp.float32
BF16 = jnp.bfloat16


def pieces(x):
    out = []
    for _ in range(3):
        part = lax.reduce_precision(x, 8, 7)
        out.append(part.astype(BF16))
        x = x - part
    return out


def joined(parts, at):
    return (
        parts[:, at].astype(F32) + parts[:, at + 1].astype(F32) + parts[:, at + 2].astype(F32)
    )


def split2(x):
    high = x.astype(BF16)
    return high, (x - high.astype(F32)).astype(BF16)


def tdot(a, b):
    return lax.dot_general(a, b, (((0,), (0,)), ((), ())), preferred_element_type=F32)


def solve_kernel(limit_steps, unit, innovation, ratio, carry, out, s2, a2, work, x, r, p, norms):
    nd, ne = unit.shape
    cols = innovation.shape[1]
    high, low = split2(unit[...].astype(F32) * ratio[...])
    s2[:nd, :] = high
    s2[nd:, :] = low
    cross = tdot(high, low)
    work[...] = cross + cross.T
    work[...] += tdot(high, high)
    for first in range(0, ne, cols):
        rows = pl.ds(first, cols)
        across = lax.broadcasted_iota(jnp.int32, (cols, ne), 1)
        down = lax.broadcasted_iota(jnp.int32, (cols, ne), 0) + first
        block = work[rows, :] + jnp.where(across == down, 1.0, 0.0)
        a_high, a_low = split2(block)
        a2[rows, :] = a_high
        a2[pl.ds(ne + first, cols), :] = a_low
    inn = innovation[...]
    rhs = tdot(high, inn) + tdot(low, inn)
    inn32 = inn.astype(F32)
    goal = jnp.sum(inn32 * inn32, axis=0, keepdims=True) * (2.0**-30)
    x[...] = jnp.zeros_like(x)
    r[...] = rhs
    p[...] = rhs
    rr0 = jnp.sum(rhs * rhs, axis=0, keepdims=True)
    norms[0:1, :] = rr0
    norms[1:2, :] = goal

    def more(state):
        step, worst = state
        return jnp.logical_and(step < limit_steps, worst > 0.0)

    def block(state):
        step, _ = state
        rr = norms[0:1, :]
        for _ in range(CHECK_EVERY):
            p_now = p[...]
            p_high, p_low = split2(p_now)
            both = jnp.dot(
                a2[...], jnp.concatenate([p_high, p_low], axis=1), preferred_element_type=F32
            )
            q = (both[:ne, :cols] + both[:ne, cols:]) + (both[ne:, :cols] + both[ne:, cols:])
            pq = jnp.sum(p_now * q, axis=0, keepdims=True)
            alpha = jnp.where(pq > 0.0, rr / jnp.where(pq > 0.0, pq, 1.0), 0.0)
            x[...] = x[...] + alpha * p_now
            r_new = r[...] - alpha * q
            r[...] = r_new
            rr_new = jnp.sum(r_new * r_new, axis=0, keepdims=True)
            beta = jnp.where(rr > 0.0, rr_new / jnp.where(rr > 0.0, rr, 1.0), 0.0)
            p[...] = r_new + beta * p_now
            rr = rr_new
        norms[0:1, :] = rr
        return step + CHECK_EVERY, jnp.max(rr - norms[1:2, :])

    lax.while_loop(more, block, (jnp.int32(0), jnp.max(rr0 - goal)))
    x_high, x_low = split2(x[...])
    both = jnp.dot(s2[...], jnp.concatenate([x_high, x_low], axis=1), preferred_element_type=F32)
    fitted = (both[:nd, :cols] + both[:nd, cols:]) + (both[nd:, :cols] + both[nd:, cols:])
    out[...] = ((inn32 - fitted) * carry[...]).astype(BF16)


def solve(unit, innovation, ratio, carry):
    nd, ne = unit.shape
    cols = innovation.shape[1]
    vmem = pl.BlockSpec(memory_space=pltpu.VMEM)
    return pl.pallas_call(
        lambda *refs: solve_kernel(8 * ne, *refs),
        out_shape=jax.ShapeDtypeStruct((nd, cols), BF16),
        in_specs=[vmem] * 4,
        out_specs=vmem,
        scratch_shapes=[
            pltpu.VMEM((2 * nd, ne), BF16),
            pltpu.VMEM((2 * ne, ne), BF16),
            pltpu.VMEM((ne, ne), F32),
            pltpu.VMEM((ne, cols), F32),
            pltpu.VMEM((ne, cols), F32),
            pltpu.VMEM((ne, cols), F32),
            pltpu.VMEM((8, cols), F32),
        ],
        compiler_params=pltpu.CompilerParams(vmem_limit_bytes=40 * 2**20),
        name="solve",
    )(unit, innovation, ratio, carry)


def gather_kernel(nz, ny, nx, unit_in, inn_in, unit_out, inn_out, held, send, recv, local):
    cores = 2
    cell, dp = lax.axis_index("cell"), lax.axis_index("dp")
    z, y = cell // ny, cell % ny
    x, core = dp // cores, dp % cores

    def z_peer(d):
        return (((z + d) % nz) * ny + y, dp)

    def x_peer(d):
        return (cell, ((x + d) % nx) * cores + core)

    def y_peer(d):
        return (z * ny + (y + d) % ny, dp)

    core_peer = (cell, x * cores + (core + 1) % cores)
    peers = [z_peer(d) for d in range(1, nz)] + [x_peer(d) for d in range(1, nx)]
    peers += [y_peer(d) for d in range(1, ny)] + [core_peer]
    barrier = pltpu.get_barrier_semaphore()
    for peer in peers:
        pl.semaphore_signal(
            barrier, inc=1, device_id=peer, device_id_type=pl.DeviceIdType.MESH
        )
    pl.semaphore_wait(barrier, len(peers))

    started = []

    def put(src, dst, peer):
        at = len(started)
        copy = pltpu.make_async_remote_copy(
            src_ref=src,
            dst_ref=dst,
            send_sem=send.at[at],
            recv_sem=recv.at[at],
            device_id=peer,
            device_id_type=pl.DeviceIdType.MESH,
        )
        copy.start()
        started.append(copy)
        return copy

    def own(slot):
        return all(k == 0 for k in slot)

    def unit_at(slot):
        return unit_in if own(slot) else unit_out.at[slot]

    def inn_at(slot, *part):
        if own(slot):
            return inn_in.at[part] if part else inn_in
        return held.at[slot + part]

    landed = {}

    def from_z(d):
        slot = (0, 0, 0, nz - d)
        landed[slot] = [
            put(unit_in, unit_out.at[slot], z_peer(d)),
            put(inn_in, held.at[slot], z_peer(d)),
        ]

    def along_x(kz):
        for d in range(1, nx):
            source, slot = (0, 0, 0, kz), (0, 0, nx - d, kz)
            landed[slot] = [
                put(unit_at(source), unit_out.at[slot], x_peer(d)),
                put(inn_at(source, d), held.at[slot + (0,)], x_peer(d)),
            ]

    def along_y(kx, kz):
        for d in range(1, ny):
            source, slot = (0, 0, kx, kz), (0, ny - d, kx, kz)
            landed[slot] = [
                put(unit_at(source), unit_out.at[slot], y_peer(d)),
                put(inn_at(source, 0), held.at[slot + (0,)], y_peer(d)),
            ]

    def to_core(ky, kx, kz):
        source, slot = (0, ky, kx, kz), (1, ky, kx, kz)
        landed[slot] = [
            put(unit_at(source), unit_out.at[slot], core_peer),
            put(inn_at(source, 0, 1), held.at[slot + (0, 0)], core_peer),
        ]

    def arrived(slot):
        if not own(slot):
            for copy in landed[slot]:
                copy.wait_recv()

    keep = [
        pltpu.make_async_copy(unit_in, unit_out.at[0, 0, 0, 0], local.at[0]),
        pltpu.make_async_copy(inn_in, held.at[0, 0, 0, 0], local.at[1]),
    ]
    for d in range(1, nz):
        from_z(d)
    for copy in keep:
        copy.start()
    for kz in range(nz):
        arrived((0, 0, 0, kz))
        along_x(kz)
        along_y(0, kz)
        to_core(0, 0, kz)
    for kx in range(1, nx):
        for kz in range(nz):
            arrived((0, 0, kx, kz))
            along_y(kx, kz)
            to_core(0, kx, kz)
    for ky in range(1, ny):
        for kx in range(nx):
            for kz in range(nz):
                arrived((0, ky, kx, kz))
                to_core(ky, kx, kz)
    for ky in range(ny):
        for kx in range(nx):
            for kz in range(nz):
                arrived((1, ky, kx, kz))
    for copy in keep:
        copy.wait()
    for copy in started:
        copy.wait_send()
    for c in range(cores):
        for ky in range(ny):
            for kx in range(nx):
                for kz in range(nz):
                    inn_out[c, ky, kx, kz] = held[c, ky, kx, kz, 0, 0]


def gather(unit, innovation):
    cells, dps = lax.axis_size("cell"), lax.axis_size("dp")
    ny = 2 if cells % 2 == 0 else 1
    nz, nx = cells // ny, dps // 2
    rows, width = unit.shape
    cols = innovation.shape[-1]
    copies = 2 * (cells * dps - 1)
    vmem = pl.BlockSpec(memory_space=pltpu.VMEM)
    units, inns = pl.pallas_call(
        lambda *refs: gather_kernel(nz, ny, nx, *refs),
        out_shape=[
            jax.ShapeDtypeStruct((2, ny, nx, nz, rows, width), BF16),
            jax.ShapeDtypeStruct((2, ny, nx, nz, rows, cols), BF16),
        ],
        in_specs=[vmem] * 2,
        out_specs=[vmem] * 2,
        scratch_shapes=[
            pltpu.VMEM((2, ny, nx, nz, nx, 2, rows, cols), BF16),
            pltpu.SemaphoreType.DMA((copies,)),
            pltpu.SemaphoreType.DMA((copies,)),
            pltpu.SemaphoreType.DMA((2,)),
        ],
        compiler_params=pltpu.CompilerParams(
            collective_id=0, has_side_effects=True, vmem_limit_bytes=40 * 2**20
        ),
        name="gather",
    )(unit, innovation)
    return units.reshape(-1, width), inns.reshape(-1, cols)


def per_device(ensemble, response_estimates, observed, obs_std, threshold):
    ne = ensemble.shape[1]
    forecast = response_estimates[0]
    observe = observed[0]
    noise_root = obs_std[0] * math.sqrt(inflation)
    deviation = forecast - jnp.mean(forecast, axis=1, keepdims=True)
    data_scale = jnp.sqrt(jnp.mean(deviation * deviation, axis=1) + 1e-06)
    unit_data = (deviation / (data_scale[:, None] * math.sqrt(ne))).astype(BF16)
    ratio = data_scale * math.sqrt(ne) / (noise_root * math.sqrt(ne - 1.0))
    carry = data_scale / noise_root
    innovation = (observe - forecast) / noise_root[:, None]
    squares = jnp.sum(innovation * innovation, axis=1)
    meta = jnp.stack(
        pieces(ratio) + pieces(carry) + pieces(squares) + [threshold[0].astype(BF16)], axis=1
    )
    meta = jnp.pad(meta, ((0, 0), (0, LANES - meta.shape[1])))
    column_count = ne // lax.axis_size("dp")
    dp = lax.axis_index("dp")
    first_col = dp * column_count
    nx = lax.axis_size("dp") // 2
    blocks = innovation.astype(BF16).reshape(-1, nx, 2, column_count).transpose(1, 2, 0, 3)
    blocks = jnp.concatenate([blocks, blocks], axis=0)
    blocks = lax.dynamic_slice_in_dim(blocks, dp // 2, nx, 0)
    blocks = jnp.concatenate([blocks, blocks], axis=1)
    blocks = lax.dynamic_slice_in_dim(blocks, dp % 2, 2, 1)
    whole, own_innovation = gather(jnp.concatenate([unit_data, meta], axis=1), blocks)
    nd = whole.shape[0]
    unit_all = whole[:, :ne]
    parts = whole[:, ne:]
    mismatch = jnp.sum(joined(parts, 6)) / (nd * ne)
    carried = solve(
        unit_all, own_innovation, joined(parts, 0)[:, None], joined(parts, 3)[:, None]
    )
    limit = parts[:, 9].astype(F32)

    values = ensemble.astype(F32)
    anomaly = values - jnp.mean(values, axis=1, keepdims=True)
    cell_scale = jnp.sqrt(jnp.mean(anomaly * anomaly, axis=1) + 1e-06)
    unit_cells = (anomaly / (cell_scale[:, None] * math.sqrt(ne))).astype(BF16)
    correlate = lax.dot_general(
        unit_cells, unit_all, (((1,), (1,)), ((), ())), preferred_element_type=F32
    )
    square = correlate * correlate
    weighted = (square / (square + (limit * limit)[None, :]) * correlate).astype(BF16)
    increment = jnp.dot(weighted, carried, preferred_element_type=F32)
    own_values = lax.dynamic_slice_in_dim(values, first_col, column_count, 1)
    updated = own_values + cell_scale[:, None] * (ne / (ne - 1.0)) * increment
    return (updated, mismatch)


def solution(mesh):
    return jax.shard_map(
        per_device,
        mesh=mesh,
        in_specs=(
            P("cell", None),
            P("dp", "cell", None),
            P("dp", "cell", None),
            P("dp", "cell"),
            P("dp", "cell"),
        ),
        out_specs=(P("cell", "dp"), P()),
        check_vma=False,
    )
```

```python
import math

import jax
import jax.numpy as jnp
from jax import lax
from jax.experimental import pallas as pl
from jax.experimental.pallas import tpu as pltpu
from jax.sharding import PartitionSpec as P

inflation = 4.0
LANES = 128
CHECK_EVERY = 3
F32 = jnp.float32
BF16 = jnp.bfloat16


def pieces(x):
    out = []
    for _ in range(3):
        part = lax.reduce_precision(x, 8, 7)
        out.append(part.astype(BF16))
        x = x - part
    return out


def joined(parts, at):
    return (
        parts[:, at].astype(F32) + parts[:, at + 1].astype(F32) + parts[:, at + 2].astype(F32)
    )


def split2(x):
    high = x.astype(BF16)
    return high, (x - high.astype(F32)).astype(BF16)


def tdot(a, b):
    return lax.dot_general(a, b, (((0,), (0,)), ((), ())), preferred_element_type=F32)


def solve_kernel(limit_steps, unit, innovation, ratio, carry, out, s2, a2, work, x, r, p, norms):
    nd, ne = unit.shape
    cols = innovation.shape[1]
    high, low = split2(unit[...].astype(F32) * ratio[...])
    s2[:nd, :] = high
    s2[nd:, :] = low
    cross = tdot(high, low)
    work[...] = cross + cross.T
    work[...] += tdot(high, high)
    for first in range(0, ne, cols):
        rows = pl.ds(first, cols)
        across = lax.broadcasted_iota(jnp.int32, (cols, ne), 1)
        down = lax.broadcasted_iota(jnp.int32, (cols, ne), 0) + first
        block = work[rows, :] + jnp.where(across == down, 1.0, 0.0)
        a_high, a_low = split2(block)
        a2[rows, :] = a_high
        a2[pl.ds(ne + first, cols), :] = a_low
    inn = innovation[...]
    rhs = tdot(high, inn) + tdot(low, inn)
    inn32 = inn.astype(F32)
    goal = jnp.sum(inn32 * inn32, axis=0, keepdims=True) * (2.0**-24)
    x[...] = jnp.zeros_like(x)
    r[...] = rhs
    p[...] = rhs
    rr0 = jnp.sum(rhs * rhs, axis=0, keepdims=True)
    norms[0:1, :] = rr0
    norms[1:2, :] = goal

    def more(state):
        step, worst = state
        return jnp.logical_and(step < limit_steps, worst > 0.0)

    def block(state):
        step, _ = state
        rr = norms[0:1, :]
        for _ in range(CHECK_EVERY):
            p_now = p[...]
            p_high, p_low = split2(p_now)
            both = jnp.dot(
                a2[...], jnp.concatenate([p_high, p_low], axis=1), preferred_element_type=F32
            )
            q = (both[:ne, :cols] + both[:ne, cols:]) + (both[ne:, :cols] + both[ne:, cols:])
            pq = jnp.sum(p_now * q, axis=0, keepdims=True)
            alpha = jnp.where(pq > 0.0, rr / jnp.where(pq > 0.0, pq, 1.0), 0.0)
            x[...] = x[...] + alpha * p_now
            r_new = r[...] - alpha * q
            r[...] = r_new
            rr_new = jnp.sum(r_new * r_new, axis=0, keepdims=True)
            beta = jnp.where(rr > 0.0, rr_new / jnp.where(rr > 0.0, rr, 1.0), 0.0)
            p[...] = r_new + beta * p_now
            rr = rr_new
        norms[0:1, :] = rr
        return step + CHECK_EVERY, jnp.max(rr - norms[1:2, :])

    lax.while_loop(more, block, (jnp.int32(0), jnp.max(rr0 - goal)))
    x_high, x_low = split2(x[...])
    both = jnp.dot(s2[...], jnp.concatenate([x_high, x_low], axis=1), preferred_element_type=F32)
    fitted = (both[:nd, :cols] + both[:nd, cols:]) + (both[nd:, :cols] + both[nd:, cols:])
    out[...] = ((inn32 - fitted) * carry[...]).astype(BF16)


def solve(unit, innovation, ratio, carry):
    nd, ne = unit.shape
    cols = innovation.shape[1]
    vmem = pl.BlockSpec(memory_space=pltpu.VMEM)
    return pl.pallas_call(
        lambda *refs: solve_kernel(8 * ne, *refs),
        out_shape=jax.ShapeDtypeStruct((nd, cols), BF16),
        in_specs=[vmem] * 4,
        out_specs=vmem,
        scratch_shapes=[
            pltpu.VMEM((2 * nd, ne), BF16),
            pltpu.VMEM((2 * ne, ne), BF16),
            pltpu.VMEM((ne, ne), F32),
            pltpu.VMEM((ne, cols), F32),
            pltpu.VMEM((ne, cols), F32),
            pltpu.VMEM((ne, cols), F32),
            pltpu.VMEM((8, cols), F32),
        ],
        compiler_params=pltpu.CompilerParams(vmem_limit_bytes=40 * 2**20),
        name="solve",
    )(unit, innovation, ratio, carry)


def gather_kernel(nz, ny, nx, unit_in, inn_in, unit_out, inn_out, held, send, recv, local):
    cores = 2
    cell, dp = lax.axis_index("cell"), lax.axis_index("dp")
    z, y = cell // ny, cell % ny
    x, core = dp // cores, dp % cores

    def z_peer(d):
        return (((z + d) % nz) * ny + y, dp)

    def x_peer(d):
        return (cell, ((x + d) % nx) * cores + core)

    def y_peer(d):
        return (z * ny + (y + d) % ny, dp)

    core_peer = (cell, x * cores + (core + 1) % cores)
    peers = [z_peer(d) for d in range(1, nz)] + [x_peer(d) for d in range(1, nx)]
    peers += [y_peer(d) for d in range(1, ny)] + [core_peer]
    barrier = pltpu.get_barrier_semaphore()
    for peer in peers:
        pl.semaphore_signal(
            barrier, inc=1, device_id=peer, device_id_type=pl.DeviceIdType.MESH
        )
    pl.semaphore_wait(barrier, len(peers))

    started = []

    def put(src, dst, peer):
        at = len(started)
        copy = pltpu.make_async_remote_copy(
            src_ref=src,
            dst_ref=dst,
            send_sem=send.at[at],
            recv_sem=recv.at[at],
            device_id=peer,
            device_id_type=pl.DeviceIdType.MESH,
        )
        copy.start()
        started.append(copy)
        return copy

    def own(slot):
        return all(k == 0 for k in slot)

    def unit_at(slot):
        return unit_in if own(slot) else unit_out.at[slot]

    def inn_at(slot, *part):
        if own(slot):
            return inn_in.at[part] if part else inn_in
        return held.at[slot + part]

    landed = {}

    def from_z(d):
        slot = (0, 0, 0, nz - d)
        landed[slot] = [
            put(unit_in, unit_out.at[slot], z_peer(d)),
            put(inn_in, held.at[slot], z_peer(d)),
        ]

    def along_x(kz):
        for d in range(1, nx):
            source, slot = (0, 0, 0, kz), (0, 0, nx - d, kz)
            landed[slot] = [
                put(unit_at(source), unit_out.at[slot], x_peer(d)),
                put(inn_at(source, d), held.at[slot + (0,)], x_peer(d)),
            ]

    def along_y(kx, kz):
        for d in range(1, ny):
            source, slot = (0, 0, kx, kz), (0, ny - d, kx, kz)
            landed[slot] = [
                put(unit_at(source), unit_out.at[slot], y_peer(d)),
                put(inn_at(source, 0), held.at[slot + (0,)], y_peer(d)),
            ]

    def to_core(ky, kx, kz):
        source, slot = (0, ky, kx, kz), (1, ky, kx, kz)
        landed[slot] = [
            put(unit_at(source), unit_out.at[slot], core_peer),
            put(inn_at(source, 0, 1), held.at[slot + (0, 0)], core_peer),
        ]

    def arrived(slot):
        if not own(slot):
            for copy in landed[slot]:
                copy.wait_recv()

    keep = [
        pltpu.make_async_copy(unit_in, unit_out.at[0, 0, 0, 0], local.at[0]),
        pltpu.make_async_copy(inn_in, held.at[0, 0, 0, 0], local.at[1]),
    ]
    for d in range(1, nz):
        from_z(d)
    for copy in keep:
        copy.start()
    for kz in range(nz):
        arrived((0, 0, 0, kz))
        along_x(kz)
        along_y(0, kz)
        to_core(0, 0, kz)
    for kx in range(1, nx):
        for kz in range(nz):
            arrived((0, 0, kx, kz))
            along_y(kx, kz)
            to_core(0, kx, kz)
    for ky in range(1, ny):
        for kx in range(nx):
            for kz in range(nz):
                arrived((0, ky, kx, kz))
                to_core(ky, kx, kz)
    for ky in range(ny):
        for kx in range(nx):
            for kz in range(nz):
                arrived((1, ky, kx, kz))
    for copy in keep:
        copy.wait()
    for copy in started:
        copy.wait_send()
    for c in range(cores):
        for ky in range(ny):
            for kx in range(nx):
                for kz in range(nz):
                    inn_out[c, ky, kx, kz] = held[c, ky, kx, kz, 0, 0]


def gather(unit, innovation):
    cells, dps = lax.axis_size("cell"), lax.axis_size("dp")
    ny = 2 if cells % 2 == 0 else 1
    nz, nx = cells // ny, dps // 2
    rows, width = unit.shape
    cols = innovation.shape[-1]
    copies = 2 * (cells * dps - 1)
    vmem = pl.BlockSpec(memory_space=pltpu.VMEM)
    units, inns = pl.pallas_call(
        lambda *refs: gather_kernel(nz, ny, nx, *refs),
        out_shape=[
            jax.ShapeDtypeStruct((2, ny, nx, nz, rows, width), BF16),
            jax.ShapeDtypeStruct((2, ny, nx, nz, rows, cols), BF16),
        ],
        in_specs=[vmem] * 2,
        out_specs=[vmem] * 2,
        scratch_shapes=[
            pltpu.VMEM((2, ny, nx, nz, nx, 2, rows, cols), BF16),
            pltpu.SemaphoreType.DMA((copies,)),
            pltpu.SemaphoreType.DMA((copies,)),
            pltpu.SemaphoreType.DMA((2,)),
        ],
        compiler_params=pltpu.CompilerParams(
            collective_id=0, has_side_effects=True, vmem_limit_bytes=40 * 2**20
        ),
        name="gather",
    )(unit, innovation)
    return units.reshape(-1, width), inns.reshape(-1, cols)


def taper_kernel(_, ensemble, own, unit, carried, limit2, out):
    ne = ensemble.shape[1]
    nd = carried.shape[0]
    values = ensemble[...].astype(F32)
    anomaly = values - jnp.mean(values, axis=1, keepdims=True)
    scale = jnp.sqrt(jnp.mean(anomaly * anomaly, axis=1, keepdims=True) + 1e-06)
    cells = (anomaly * (1.0 / (scale * math.sqrt(ne)))).astype(BF16)
    step = 256 if nd % 256 == 0 else nd
    total = jnp.zeros(out.shape, F32)
    for first in range(0, nd, step):
        rows = slice(first, first + step)
        correlate = lax.dot_general(
            cells, unit[rows, :ne], (((1,), (1,)), ((), ())), preferred_element_type=F32
        )
        square = correlate * correlate
        weighted = (square / (square + limit2[:, rows]) * correlate).astype(BF16)
        total = total + jnp.dot(weighted, carried[rows, :], preferred_element_type=F32)
    out[...] = own[...].astype(F32) + scale * (ne / (ne - 1.0)) * total


def taper(dp, ensemble, unit, carried, limit2):
    rows, ne = ensemble.shape
    nd, cols = carried.shape
    block = 512 if rows % 512 == 0 else rows
    return pl.pallas_call(
        taper_kernel,
        grid_spec=pltpu.PrefetchScalarGridSpec(
            num_scalar_prefetch=1,
            grid=(rows // block,),
            in_specs=[
                pl.BlockSpec((block, ne), lambda i, at: (i, 0)),
                pl.BlockSpec((block, cols), lambda i, at: (i, at[0])),
                pl.BlockSpec(unit.shape, lambda i, at: (0, 0)),
                pl.BlockSpec((nd, cols), lambda i, at: (0, 0)),
                pl.BlockSpec((1, nd), lambda i, at: (0, 0)),
            ],
            out_specs=pl.BlockSpec((block, cols), lambda i, at: (i, 0)),
        ),
        out_shape=jax.ShapeDtypeStruct((rows, cols), F32),
        compiler_params=pltpu.CompilerParams(vmem_limit_bytes=40 * 2**20),
        name="taper",
    )(dp.reshape(1).astype(jnp.int32), ensemble, ensemble, unit, carried, limit2)


def per_device(ensemble, response_estimates, observed, obs_std, threshold):
    ne = ensemble.shape[1]
    forecast = response_estimates[0]
    observe = observed[0]
    noise_root = obs_std[0] * math.sqrt(inflation)
    deviation = forecast - jnp.mean(forecast, axis=1, keepdims=True)
    data_scale = jnp.sqrt(jnp.mean(deviation * deviation, axis=1) + 1e-06)
    unit_data = (deviation / (data_scale[:, None] * math.sqrt(ne))).astype(BF16)
    ratio = data_scale * math.sqrt(ne) / (noise_root * math.sqrt(ne - 1.0))
    carry = data_scale / noise_root
    innovation = (observe - forecast) / noise_root[:, None]
    squares = jnp.sum(innovation * innovation, axis=1)
    meta = jnp.stack(
        pieces(ratio) + pieces(carry) + pieces(squares) + [threshold[0].astype(BF16)], axis=1
    )
    meta = jnp.pad(meta, ((0, 0), (0, LANES - meta.shape[1])))
    column_count = ne // lax.axis_size("dp")
    dp = lax.axis_index("dp")
    nx = lax.axis_size("dp") // 2
    blocks = innovation.astype(BF16).reshape(-1, nx, 2, column_count).transpose(1, 2, 0, 3)
    blocks = jnp.concatenate([blocks, blocks], axis=0)
    blocks = lax.dynamic_slice_in_dim(blocks, dp // 2, nx, 0)
    blocks = jnp.concatenate([blocks, blocks], axis=1)
    blocks = lax.dynamic_slice_in_dim(blocks, dp % 2, 2, 1)
    whole, own_innovation = gather(jnp.concatenate([unit_data, meta], axis=1), blocks)
    nd = whole.shape[0]
    unit_all = whole[:, :ne]
    parts = whole[:, ne:]
    mismatch = jnp.sum(joined(parts, 6)) / (nd * ne)
    carried = solve(
        unit_all, own_innovation, joined(parts, 0)[:, None], joined(parts, 3)[:, None]
    )
    limit = parts[:, 9].astype(F32)

    updated = taper(dp, ensemble, whole, carried, (limit * limit)[None, :])
    return (updated, mismatch)


def solution(mesh):
    return jax.shard_map(
        per_device,
        mesh=mesh,
        in_specs=(
            P("cell", None),
            P("dp", "cell", None),
            P("dp", "cell", None),
            P("dp", "cell"),
            P("dp", "cell"),
        ),
        out_specs=(P("cell", "dp"), P()),
        check_vma=False,
    )
```

```python
import math

import jax
import jax.numpy as jnp
from jax import lax
from jax.experimental import pallas as pl
from jax.experimental.pallas import tpu as pltpu
from jax.sharding import PartitionSpec as P

inflation = 4.0
LANES = 128
CHECK_EVERY = 3
F32 = jnp.float32
BF16 = jnp.bfloat16


def pieces(x):
    out = []
    for _ in range(3):
        part = lax.reduce_precision(x, 8, 7)
        out.append(part.astype(BF16))
        x = x - part
    return out


def joined(parts, at):
    return (
        parts[:, at].astype(F32) + parts[:, at + 1].astype(F32) + parts[:, at + 2].astype(F32)
    )


def split2(x):
    high = x.astype(BF16)
    return high, (x - high.astype(F32)).astype(BF16)


def tdot(a, b):
    return lax.dot_general(a, b, (((0,), (0,)), ((), ())), preferred_element_type=F32)


def solve_kernel(limit_steps, unit, innovation, ratio, carry, out, s2, a2, work, x, r, p, norms):
    nd, ne = unit.shape
    cols = innovation.shape[1]
    high, low = split2(unit[...].astype(F32) * ratio[...])
    s2[:nd, :] = high
    s2[nd:, :] = low
    cross = tdot(high, low)
    work[...] = cross + cross.T
    work[...] += tdot(high, high)
    for first in range(0, ne, cols):
        rows = pl.ds(first, cols)
        across = lax.broadcasted_iota(jnp.int32, (cols, ne), 1)
        down = lax.broadcasted_iota(jnp.int32, (cols, ne), 0) + first
        block = work[rows, :] + jnp.where(across == down, 1.0, 0.0)
        a_high, a_low = split2(block)
        a2[rows, :] = a_high
        a2[pl.ds(ne + first, cols), :] = a_low
    inn = innovation[...]
    rhs = tdot(high, inn) + tdot(low, inn)
    inn32 = inn.astype(F32)
    goal = jnp.sum(inn32 * inn32, axis=0, keepdims=True) * (2.0**-24)
    rr0 = jnp.sum(rhs * rhs, axis=0, keepdims=True)

    def coarse(v):
        return jnp.dot(a2[:ne, :], v.astype(BF16), preferred_element_type=F32)

    def full(v):
        v_high, v_low = split2(v)
        both = jnp.dot(
            a2[:ne, :], jnp.concatenate([v_high, v_low], axis=1), preferred_element_type=F32
        )
        return (both[:, :cols] + both[:, cols:]) + jnp.dot(
            a2[ne:, :], v_high, preferred_element_type=F32
        )

    def run(operator, residual, rr_first, bound, limit):
        r[...] = residual
        p[...] = residual
        norms[0:1, :] = rr_first
        norms[1:2, :] = bound

        def more(state):
            step, worst = state
            return jnp.logical_and(step < limit, worst > 0.0)

        def block(state):
            step, _ = state
            rr = norms[0:1, :]
            for _ in range(CHECK_EVERY):
                p_now = p[...]
                q = operator(p_now)
                pq = jnp.sum(p_now * q, axis=0, keepdims=True)
                alpha = jnp.where(pq > 0.0, rr / jnp.where(pq > 0.0, pq, 1.0), 0.0)
                x[...] = x[...] + alpha * p_now
                r_new = r[...] - alpha * q
                r[...] = r_new
                rr_new = jnp.sum(r_new * r_new, axis=0, keepdims=True)
                beta = jnp.where(rr > 0.0, rr_new / jnp.where(rr > 0.0, rr, 1.0), 0.0)
                p[...] = r_new + beta * p_now
                rr = rr_new
            norms[0:1, :] = rr
            return step + CHECK_EVERY, jnp.max(rr - norms[1:2, :])

        lax.while_loop(more, block, (jnp.int32(0), jnp.max(rr_first - bound)))

    x[...] = jnp.zeros_like(x)
    run(coarse, rhs, rr0, goal * (2.0**12), min(24, limit_steps))
    left = rhs - full(x[...])
    rr1 = jnp.sum(left * left, axis=0, keepdims=True)
    useful = rr1 < rr0
    x[...] = jnp.where(useful, x[...], 0.0)
    run(full, jnp.where(useful, left, rhs), jnp.where(useful, rr1, rr0), goal, limit_steps)
    x_high, x_low = split2(x[...])
    both = jnp.dot(s2[...], jnp.concatenate([x_high, x_low], axis=1), preferred_element_type=F32)
    fitted = (both[:nd, :cols] + both[:nd, cols:]) + (both[nd:, :cols] + both[nd:, cols:])
    out[...] = ((inn32 - fitted) * carry[...]).astype(BF16)


def solve(unit, innovation, ratio, carry):
    nd, ne = unit.shape
    cols = innovation.shape[1]
    vmem = pl.BlockSpec(memory_space=pltpu.VMEM)
    return pl.pallas_call(
        lambda *refs: solve_kernel(8 * ne, *refs),
        out_shape=jax.ShapeDtypeStruct((nd, cols), BF16),
        in_specs=[vmem] * 4,
        out_specs=vmem,
        scratch_shapes=[
            pltpu.VMEM((2 * nd, ne), BF16),
            pltpu.VMEM((2 * ne, ne), BF16),
            pltpu.VMEM((ne, ne), F32),
            pltpu.VMEM((ne, cols), F32),
            pltpu.VMEM((ne, cols), F32),
            pltpu.VMEM((ne, cols), F32),
            pltpu.VMEM((8, cols), F32),
        ],
        compiler_params=pltpu.CompilerParams(vmem_limit_bytes=40 * 2**20),
        name="solve",
    )(unit, innovation, ratio, carry)


def gather_kernel(nz, ny, nx, unit_in, inn_in, unit_out, inn_out, held, send, recv, local):
    cores = 2
    cell, dp = lax.axis_index("cell"), lax.axis_index("dp")
    z, y = cell // ny, cell % ny
    x, core = dp // cores, dp % cores

    def z_peer(d):
        return (((z + d) % nz) * ny + y, dp)

    def x_peer(d):
        return (cell, ((x + d) % nx) * cores + core)

    def y_peer(d):
        return (z * ny + (y + d) % ny, dp)

    core_peer = (cell, x * cores + (core + 1) % cores)
    peers = [z_peer(d) for d in range(1, nz)] + [x_peer(d) for d in range(1, nx)]
    peers += [y_peer(d) for d in range(1, ny)] + [core_peer]
    barrier = pltpu.get_barrier_semaphore()
    for peer in peers:
        pl.semaphore_signal(
            barrier, inc=1, device_id=peer, device_id_type=pl.DeviceIdType.MESH
        )
    pl.semaphore_wait(barrier, len(peers))

    started = []

    def put(src, dst, peer):
        at = len(started)
        copy = pltpu.make_async_remote_copy(
            src_ref=src,
            dst_ref=dst,
            send_sem=send.at[at],
            recv_sem=recv.at[at],
            device_id=peer,
            device_id_type=pl.DeviceIdType.MESH,
        )
        copy.start()
        started.append(copy)
        return copy

    def own(slot):
        return all(k == 0 for k in slot)

    def unit_at(slot):
        return unit_in if own(slot) else unit_out.at[slot]

    def inn_at(slot, *part):
        if own(slot):
            return inn_in.at[part] if part else inn_in
        return held.at[slot + part]

    landed = {}

    def from_z(d):
        slot = (0, 0, 0, nz - d)
        landed[slot] = [
            put(unit_in, unit_out.at[slot], z_peer(d)),
            put(inn_in, held.at[slot], z_peer(d)),
        ]

    def along_x(kz):
        for d in range(1, nx):
            source, slot = (0, 0, 0, kz), (0, 0, nx - d, kz)
            landed[slot] = [
                put(unit_at(source), unit_out.at[slot], x_peer(d)),
                put(inn_at(source, d), held.at[slot + (0,)], x_peer(d)),
            ]

    def along_y(kx, kz):
        for d in range(1, ny):
            source, slot = (0, 0, kx, kz), (0, ny - d, kx, kz)
            landed[slot] = [
                put(unit_at(source), unit_out.at[slot], y_peer(d)),
                put(inn_at(source, 0), held.at[slot + (0,)], y_peer(d)),
            ]

    def to_core(ky, kx, kz):
        source, slot = (0, ky, kx, kz), (1, ky, kx, kz)
        landed[slot] = [
            put(unit_at(source), unit_out.at[slot], core_peer),
            put(inn_at(source, 0, 1), held.at[slot + (0, 0)], core_peer),
        ]

    def arrived(slot):
        if not own(slot):
            for copy in landed[slot]:
                copy.wait_recv()

    keep = [
        pltpu.make_async_copy(unit_in, unit_out.at[0, 0, 0, 0], local.at[0]),
        pltpu.make_async_copy(inn_in, held.at[0, 0, 0, 0], local.at[1]),
    ]
    for d in range(1, nz):
        from_z(d)
    for copy in keep:
        copy.start()
    for kz in range(nz):
        arrived((0, 0, 0, kz))
        along_x(kz)
        along_y(0, kz)
        to_core(0, 0, kz)
    for kx in range(1, nx):
        for kz in range(nz):
            arrived((0, 0, kx, kz))
            along_y(kx, kz)
            to_core(0, kx, kz)
    for ky in range(1, ny):
        for kx in range(nx):
            for kz in range(nz):
                arrived((0, ky, kx, kz))
                to_core(ky, kx, kz)
    for ky in range(ny):
        for kx in range(nx):
            for kz in range(nz):
                arrived((1, ky, kx, kz))
    for copy in keep:
        copy.wait()
    for copy in started:
        copy.wait_send()
    for c in range(cores):
        for ky in range(ny):
            for kx in range(nx):
                for kz in range(nz):
                    inn_out[c, ky, kx, kz] = held[c, ky, kx, kz, 0, 0]


def gather(unit, innovation):
    cells, dps = lax.axis_size("cell"), lax.axis_size("dp")
    ny = 2 if cells % 2 == 0 else 1
    nz, nx = cells // ny, dps // 2
    rows, width = unit.shape
    cols = innovation.shape[-1]
    copies = 2 * (cells * dps - 1)
    vmem = pl.BlockSpec(memory_space=pltpu.VMEM)
    units, inns = pl.pallas_call(
        lambda *refs: gather_kernel(nz, ny, nx, *refs),
        out_shape=[
            jax.ShapeDtypeStruct((2, ny, nx, nz, rows, width), BF16),
            jax.ShapeDtypeStruct((2, ny, nx, nz, rows, cols), BF16),
        ],
        in_specs=[vmem] * 2,
        out_specs=[vmem] * 2,
        scratch_shapes=[
            pltpu.VMEM((2, ny, nx, nz, nx, 2, rows, cols), BF16),
            pltpu.SemaphoreType.DMA((copies,)),
            pltpu.SemaphoreType.DMA((copies,)),
            pltpu.SemaphoreType.DMA((2,)),
        ],
        compiler_params=pltpu.CompilerParams(
            collective_id=0, has_side_effects=True, vmem_limit_bytes=40 * 2**20
        ),
        name="gather",
    )(unit, innovation)
    return units.reshape(-1, width), inns.reshape(-1, cols)


def taper_kernel(_, ensemble, own, unit, carried, limit2, out):
    ne = ensemble.shape[1]
    nd = carried.shape[0]
    values = ensemble[...].astype(F32)
    anomaly = values - jnp.mean(values, axis=1, keepdims=True)
    scale = jnp.sqrt(jnp.mean(anomaly * anomaly, axis=1, keepdims=True) + 1e-06)
    cells = (anomaly * (1.0 / (scale * math.sqrt(ne)))).astype(BF16)
    step = 256 if nd % 256 == 0 else nd
    total = jnp.zeros(out.shape, F32)
    for first in range(0, nd, step):
        rows = slice(first, first + step)
        correlate = lax.dot_general(
            cells, unit[rows, :ne], (((1,), (1,)), ((), ())), preferred_element_type=F32
        )
        square = correlate * correlate
        weighted = (square / (square + limit2[:, rows]) * correlate).astype(BF16)
        total = total + jnp.dot(weighted, carried[rows, :], preferred_element_type=F32)
    out[...] = own[...].astype(F32) + scale * (ne / (ne - 1.0)) * total


def taper(dp, ensemble, unit, carried, limit2):
    rows, ne = ensemble.shape
    nd, cols = carried.shape
    block = 512 if rows % 512 == 0 else rows
    return pl.pallas_call(
        taper_kernel,
        grid_spec=pltpu.PrefetchScalarGridSpec(
            num_scalar_prefetch=1,
            grid=(rows // block,),
            in_specs=[
                pl.BlockSpec((block, ne), lambda i, at: (i, 0)),
                pl.BlockSpec((block, cols), lambda i, at: (i, at[0])),
                pl.BlockSpec(unit.shape, lambda i, at: (0, 0)),
                pl.BlockSpec((nd, cols), lambda i, at: (0, 0)),
                pl.BlockSpec((1, nd), lambda i, at: (0, 0)),
            ],
            out_specs=pl.BlockSpec((block, cols), lambda i, at: (i, 0)),
        ),
        out_shape=jax.ShapeDtypeStruct((rows, cols), F32),
        compiler_params=pltpu.CompilerParams(vmem_limit_bytes=40 * 2**20),
        name="taper",
    )(dp.reshape(1).astype(jnp.int32), ensemble, ensemble, unit, carried, limit2)


def per_device(ensemble, response_estimates, observed, obs_std, threshold):
    ne = ensemble.shape[1]
    forecast = response_estimates[0]
    observe = observed[0]
    noise_root = obs_std[0] * math.sqrt(inflation)
    deviation = forecast - jnp.mean(forecast, axis=1, keepdims=True)
    data_scale = jnp.sqrt(jnp.mean(deviation * deviation, axis=1) + 1e-06)
    unit_data = (deviation / (data_scale[:, None] * math.sqrt(ne))).astype(BF16)
    ratio = data_scale * math.sqrt(ne) / (noise_root * math.sqrt(ne - 1.0))
    carry = data_scale / noise_root
    innovation = (observe - forecast) / noise_root[:, None]
    squares = jnp.sum(innovation * innovation, axis=1)
    meta = jnp.stack(
        pieces(ratio) + pieces(carry) + pieces(squares) + [threshold[0].astype(BF16)], axis=1
    )
    meta = jnp.pad(meta, ((0, 0), (0, LANES - meta.shape[1])))
    column_count = ne // lax.axis_size("dp")
    dp = lax.axis_index("dp")
    nx = lax.axis_size("dp") // 2
    blocks = innovation.astype(BF16).reshape(-1, nx, 2, column_count).transpose(1, 2, 0, 3)
    blocks = jnp.concatenate([blocks, blocks], axis=0)
    blocks = lax.dynamic_slice_in_dim(blocks, dp // 2, nx, 0)
    blocks = jnp.concatenate([blocks, blocks], axis=1)
    blocks = lax.dynamic_slice_in_dim(blocks, dp % 2, 2, 1)
    whole, own_innovation = gather(jnp.concatenate([unit_data, meta], axis=1), blocks)
    nd = whole.shape[0]
    unit_all = whole[:, :ne]
    parts = whole[:, ne:]
    mismatch = jnp.sum(joined(parts, 6)) / (nd * ne)
    carried = solve(
        unit_all, own_innovation, joined(parts, 0)[:, None], joined(parts, 3)[:, None]
    )
    limit = parts[:, 9].astype(F32)

    updated = taper(dp, ensemble, whole, carried, (limit * limit)[None, :])
    return (updated, mismatch)


def solution(mesh):
    return jax.shard_map(
        per_device,
        mesh=mesh,
        in_specs=(
            P("cell", None),
            P("dp", "cell", None),
            P("dp", "cell", None),
            P("dp", "cell"),
            P("dp", "cell"),
        ),
        out_specs=(P("cell", "dp"), P()),
        check_vma=False,
    )
```
